32 devices in a mesh: groups: 2 (over x), expert: 16 (over z, y, core).
Axes of the slice: x: 2, y: 2, z: 4, core: 2. Of those that a mesh axis runs over, the one named last changes fastest.
Arguments:
- tokens: bfloat16 [8192, 1024], P(('groups', 'expert')), parts along dimension 0, may hold values from -6 to 6
- routes: int32 [8192, 2], P(('groups', 'expert')), parts along dimension 0, may hold values from 0 to 7, all different within a row; in each aligned block of 256 rows (0 to 255, 256 to 511, ...) at most 128 rows name the same one
- gates: float32 [8192, 2], P(('groups', 'expert')), parts along dimension 0, may hold values from 0.2 to 1
- w_in: bfloat16 [16, 1024, 2048], P('expert'), may hold values from -0.1875 to 0.1875
- w_down: bfloat16 [16, 1024, 1024], P('expert'), may hold values from -0.125 to 0.125
Outputs:
- mixed: bfloat16 [8192, 1024], P(('groups', 'expert')), parts along dimension 0
The draws below stay inside these ranges and needn't reach their ends.
There are 2 independent parts, one for each index of `groups`. The reference program is written for one: setup_inputs(seed, part) draws one part's arguments, and reference() takes and returns one part's arrays. A program takes and returns all parts, laid end to end along the dimension named above; an argument that names none is the same for every part. Nothing has to cross between parts.
Inputs may be any that keep to these rules, and one draw needn't show every extreme that they name: `routes`: each row names 2 different experts; in the 256 rows of one device no expert is named by more than 128 rows, and exactly 128 for some expert in some device's rows.
All inputs are finite; a program needn't handle non-finite values.
Results may differ from the reference program's by a relative error of at most 0.005.
Values may be sent and summed in bfloat16 or wider, within the bound.
No kernel may reach another device: no remote copies, remote signals or barrier semaphores. Data moves between devices by JAX's collectives and lax.ppermute only.
A program may use at most 64 MiB of HBM per device.

```python
import math
import jax
import jax.numpy as jnp
import numpy as np
from jax import lax

D = 1024
FF = 2048
TOP = 2
TOK_DEV = 256
HALF = 1024
EXPERTS = 8
SLICES = 16
CAP = 128
TOKENS = 4096


def level_of(rng, dims, pieces, smallest, high):
    level, own = 1.0, jax.random.fold_in(rng, 6)
    for axis_at, parts in pieces:
        draws = jnp.exp(jax.random.uniform(jax.random.fold_in(own, axis_at), (parts,), jnp.float32, smallest / len(pieces), high / len(pieces)))
        level = level * jnp.repeat(draws, dims[axis_at] // parts).reshape([-1 if axis == axis_at else 1 for axis in range(len(dims))])
    return level


def shared_out(own_key, own, number, rows, number_of, top, bound, lean):
    order = jax.random.permutation(own_key, number_of)
    heavy_load, usual = shares(number_of, rows * top, bound, lean, True), shares(number_of, rows * top, bound, lean, False)
    places = jnp.arange(number_of)

    def named(sizes, turn):
        used = int((sizes > 0).sum())
        fixed = max(1, used // 4)
        moved = fixed + (places - fixed + turn * (used - fixed)) % max(1, number_of - fixed)
        return jnp.zeros((number_of,), jnp.int32).at[order[jnp.where(places < fixed, places, moved)]].set(jnp.asarray(sizes, jnp.int32))

    sizes = jnp.where(number % 4 == 0, named(heavy_load, number // 4), named(usual, number - number // 4 - 1))
    mixed = jax.random.permutation(jax.random.fold_in(own, 3), number_of)
    source_of, taker = mixed[0:number_of // 2 * 2:2], mixed[1:number_of // 2 * 2:2]
    slack = jnp.minimum(sizes[source_of] - 1, bound - sizes[taker]) // 2
    slack = jnp.where((source_of == order[0]) | (taker == order[0]) | (sizes[taker] == 0), 0, jnp.maximum(slack, 0))
    moved = jax.random.randint(jax.random.fold_in(own, 4), (number_of // 2,), 0, 1 << 20) % (slack + 1)
    sizes = sizes.at[source_of].add(-moved).at[taker].add(moved)
    labels = jnp.searchsorted(jnp.cumsum(sizes), jnp.arange(rows * top), side="right").astype(jnp.int32)
    grid = labels.reshape(top, rows).T
    grid = grid[jax.random.permutation(jax.random.fold_in(own, 1), rows)]
    turn = jax.random.randint(jax.random.fold_in(own, 2), (rows, 1), 0, top)
    return jnp.take_along_axis(grid, (jnp.arange(top)[None, :] + turn) % top, axis=1)


def shares(amount, total, bound, slope, full):
    loads = [(1 << 20) // math.isqrt(standing ** slope) + 1 for standing in range(1, amount + 1)]
    largest = bound if full else min(bound, max(-(-total // amount), total * loads[0] // sum(loads)))
    least = 1 if total - largest >= amount - 1 else 0
    given, surplus = [largest] + [least] * (amount - 1), total - largest - least * (amount - 1)
    while surplus > 0:
        movable = [i for i in range(1, amount) if given[i] < largest] or [i for i in range(1, amount) if given[i] < bound]
        mass, left = sum([loads[i] for i in movable]), surplus
        for i in movable:
            addition = min(bound - given[i], max(1, left * loads[i] // mass), surplus)
            given[i] = given[i] + addition
            surplus = surplus - addition
    return np.array(given)


def scatter_about(key, shape, deviation, limit, shards=(), kind=jnp.bfloat16):
    entries = deviation * jax.random.normal(key, shape, jnp.float32)
    if shards:
        entries = entries * level_of(key, shape, shards, -0.22, 0.18)
    return jnp.clip(entries, -limit, limit).astype(kind)


def setup_inputs(seed: int = 0, part: int = 0) -> dict:
    keys = jax.random.split(jax.random.key(seed), 6)
    part_splits = jax.random.split(jax.random.fold_in(keys[5], part), 6)
    tokens = scatter_about(part_splits[0], (TOKENS, D), 1.0, 6.0, ((0, 16),))
    routes_keys = jax.random.split(jax.random.fold_in(part_splits[1], 1), TOKENS // TOK_DEV)
    routes_turns = jax.random.permutation(jax.random.fold_in(part_splits[1], 3), TOKENS // TOK_DEV)
    routes = jax.vmap(lambda own, number: shared_out(jax.random.fold_in(part_splits[1], 2), own, number, TOK_DEV, EXPERTS, TOP, CAP, 2))(routes_keys, routes_turns).reshape((TOKENS, TOP))
    gates = jnp.clip(0.2 + 0.8 * jax.random.uniform(part_splits[2], (TOKENS, TOP), jnp.float32) ** level_of(part_splits[2], (TOKENS, TOP), ((0, 16),), -0.2, 0.2), 0.2, 1.0)
    w_in = scatter_about(keys[3], (SLICES, D, 2 * HALF), D ** -0.5, 0.1875, ((0, 16),))
    w_down = scatter_about(keys[4], (SLICES, HALF, D), FF ** -0.5, 0.125, ((0, 16),))
    return dict(tokens=tokens, routes=routes, gates=gates, w_in=w_in, w_down=w_down)


def reference(tokens, routes, gates, w_in, w_down):
    token_count, features = tokens.shape
    half_units = w_down.shape[1]
    experts = w_in.shape[0] // 2
    route_ids = routes.reshape(-1).astype(jnp.int32)
    route_count = route_ids.shape[0]
    order = jnp.argsort(route_ids, stable=True).astype(jnp.int32)
    sorted_ids = route_ids[order]
    expert_range = jnp.arange(experts, dtype=jnp.int32)
    counts = jnp.sum((route_ids[:, None] == expert_range[None, :]).astype(jnp.int32), axis=0)
    padded = ((counts + 127) // 128) * 128
    ends = jnp.cumsum(padded).astype(jnp.int32)
    starts = ends - padded
    raw_starts = (jnp.cumsum(counts) - counts).astype(jnp.int32)
    rank = jnp.arange(route_count, dtype=jnp.int32) - raw_starts[sorted_ids]
    position = (starts[sorted_ids] + rank).astype(jnp.int32)
    blocks = route_count // 128 + experts + 1
    table = jnp.zeros((blocks * 128,), jnp.int32).at[position].set(order // 2)
    block_starts = jnp.arange(blocks, dtype=jnp.int32) * 128
    block_expert = jnp.sum((ends[None, :] <= block_starts[:, None]).astype(jnp.int32), axis=1)
    block_expert = jnp.minimum(block_expert, experts - 1).astype(jnp.int32)

    def run_block(pair):
        block_index, expert_id = pair
        picks = lax.dynamic_slice(table, (block_index * 128,), (128,))
        incoming = tokens[picks]
        total = jnp.zeros((128, features), jnp.float32)
        for half_index in range(2):
            slice_index = 2 * expert_id + half_index
            gate_up = jnp.dot(incoming, w_in[slice_index], preferred_element_type=jnp.float32)
            hidden = (jax.nn.silu(gate_up[:, :half_units]) * gate_up[:, half_units:]).astype(jnp.bfloat16)
            total = total + jnp.dot(hidden, w_down[slice_index], preferred_element_type=jnp.float32)
        return total.astype(jnp.bfloat16)

    outputs = lax.map(run_block, (jnp.arange(blocks, dtype=jnp.int32), block_expert))
    outputs = outputs.reshape(blocks * 128, features)
    route_position = jnp.zeros((route_count,), jnp.int32).at[order].set(position)
    picked = outputs[route_position].astype(jnp.float32).reshape(token_count, 2, features)
    branch = jnp.sum(gates[:, :, None] * picked, axis=1)
    return (tokens.astype(jnp.float32) + branch).astype(jnp.bfloat16)
```

```python
import functools
import jax
import jax.numpy as jnp
from jax import lax
from jax.experimental import pallas as pl
from jax.experimental.pallas import tpu as pltpu
from jax.sharding import PartitionSpec as P


F32 = jnp.float32
BF16 = jnp.bfloat16
HIDDEN_BLOCK = 512


def iota(shape, dim):
    return lax.broadcasted_iota(jnp.int32, shape, dim)


def slot_rows(routes, experts, cap):
    count = routes.shape[1]
    first, second = routes[0:1, :], routes[1:2, :]
    ids = iota((experts, count), 0)
    is_first, is_second = ids == first, ids == second
    named = jnp.where(is_first | is_second, 1.0, 0.0).astype(BF16)
    before = jnp.where(iota((count, count), 0) < iota((count, count), 1), 1.0, 0.0).astype(BF16)
    ranks = jnp.dot(named, before, preferred_element_type=F32)
    rank_first = jnp.sum(jnp.where(is_first, ranks, 0.0), axis=0, keepdims=True)
    rank_second = jnp.sum(jnp.where(is_second, ranks, 0.0), axis=0, keepdims=True)
    return first * cap + rank_first.astype(jnp.int32), second * cap + rank_second.astype(jnp.int32)


class Plan:
    def __init__(self, devices, tok_rows):
        self.devices = devices
        self.experts = devices // 2
        self.cap = min(tok_rows, 4 * tok_rows // self.experts)
        self.near = self.experts // 2
        self.direct = self.near <= 8
        self.pieces = self.near if self.direct else 1
        self.piece_rows = self.near * self.cap // self.pieces

    def bases(self):
        me = lax.axis_index("expert")
        chip = me // 2
        half_first = chip // self.near * self.near
        if not self.direct:
            return [half_first * self.cap]
        return [(half_first + ((chip % self.near) ^ j)) * self.cap for j in range(self.pieces)]

    def across(self, x):
        return lax.ppermute(x, "expert", [(i, i ^ self.devices // 2) for i in range(self.devices)])

    def partner(self, x):
        return lax.ppermute(x, "expert", [(i, i ^ 1) for i in range(self.devices)])

    def near_exchange(self, parts):
        if self.direct:
            return [parts[0]] + [
                lax.ppermute(parts[j], "expert", [(i, i ^ 2 * j) for i in range(self.devices)])
                for j in range(1, self.pieces)
            ]
        groups = [
            [2 * (half * self.near + chip) + core for chip in range(self.near)]
            for half in range(2)
            for core in range(2)
        ]
        return [lax.all_to_all(parts[0], "expert", split_axis=0, concat_axis=0, tiled=True, axis_index_groups=groups)]


def select_body(plan, routes_ref, tokens_ref, *out_refs):
    first, second = slot_rows(routes_ref[...], plan.experts, plan.cap)
    tokens = tokens_ref[...]
    slots = iota((plan.piece_rows, tokens.shape[0]), 0)
    for base, out_ref in zip(plan.bases(), out_refs):
        pick = jnp.where((slots == first - base) | (slots == second - base), 1.0, 0.0).astype(BF16)
        out_ref[...] = jnp.dot(pick, tokens, preferred_element_type=F32).astype(BF16)


def select(plan, routes, tokens):
    features = tokens.shape[1]
    return pl.pallas_call(
        functools.partial(select_body, plan),
        out_shape=[jax.ShapeDtypeStruct((plan.piece_rows, features), BF16)] * plan.pieces,
        name="select",
    )(routes, tokens)


def gated_sum(plan, routes, gates, parts):
    count = routes.shape[1]
    first, second = slot_rows(routes, plan.experts, plan.cap)
    rows = jnp.concatenate(
        [first.astype(F32), second.astype(F32), gates, jnp.zeros((124, count), F32)], axis=0
    )
    columns = rows.T
    first_col = columns[:, 0:1].astype(jnp.int32)
    second_col = columns[:, 1:2].astype(jnp.int32)
    slots = iota((count, plan.piece_rows), 1)
    bases = plan.bases()

    def picked(column):
        pick = jnp.concatenate(
            [jnp.where(slots == column - base, 1.0, 0.0).astype(BF16) for base in bases], axis=1
        )
        return jnp.dot(pick, parts, preferred_element_type=F32)

    return columns[:, 2:3] * picked(first_col) + columns[:, 3:4] * picked(second_col)


def relay_body(plan, routes_ref, gates_ref, *refs):
    parts = jnp.concatenate([ref[...] for ref in refs[:-1]], axis=0)
    refs[-1][...] = gated_sum(plan, routes_ref[...], gates_ref[...], parts).astype(BF16)


def relay_sum(plan, routes, gates, parts):
    return pl.pallas_call(
        functools.partial(relay_body, plan),
        out_shape=jax.ShapeDtypeStruct((routes.shape[1], parts[0].shape[1]), BF16),
        name="relay_sum",
    )(routes, gates, *parts)


def final_body(plan, routes_ref, gates_ref, tokens_ref, far_ref, *refs):
    parts = jnp.concatenate([ref[...] for ref in refs[:-1]], axis=0)
    branch = gated_sum(plan, routes_ref[...], gates_ref[...], parts) + far_ref[...].astype(F32)
    refs[-1][...] = (tokens_ref[...].astype(F32) + branch).astype(BF16)


def final_sum(plan, routes, gates, tokens, far, parts):
    return pl.pallas_call(
        functools.partial(final_body, plan),
        out_shape=jax.ShapeDtypeStruct(tokens.shape, BF16),
        name="final_sum",
    )(routes, gates, tokens, far, *parts)


def expert_body(count, steps, *refs):
    parts, refs = refs[:count], refs[count:]
    (gate_a, up_a, down_a, gate_b, up_b, down_b), refs = refs[:6], refs[6:]
    outs, (rows_ref, acc_ref) = refs[:count], refs[count:]
    step = pl.program_id(0)
    size = parts[0].shape[0]

    @pl.when(step == 0)
    def _():
        for j, part in enumerate(parts):
            rows_ref[j * size : (j + 1) * size, :] = part[...]

    def block(gate_ref, up_ref, down_ref):
        rows = rows_ref[...]
        gate = jnp.dot(rows, gate_ref[0], preferred_element_type=F32)
        up = jnp.dot(rows, up_ref[0], preferred_element_type=F32)
        hidden = (jax.nn.silu(gate) * up).astype(BF16)
        return jnp.dot(hidden, down_ref[0], preferred_element_type=F32)

    @pl.when(step == 0)
    def _():
        acc_ref[...] = block(gate_a, up_a, down_a)

    @pl.when((step > 0) & (step < steps))
    def _():
        acc_ref[...] += block(gate_a, up_a, down_a)

    @pl.when(step >= steps)
    def _():
        acc_ref[...] += block(gate_b, up_b, down_b)

    @pl.when(step == 2 * steps - 1)
    def _():
        for j, out in enumerate(outs):
            out[...] = acc_ref[j * size : (j + 1) * size, :].astype(BF16)


def expert(parts, weights):
    w_in, w_down, other_in, other_down = weights
    size, features = parts[0].shape
    half_units = w_down.shape[1]
    block = min(HIDDEN_BLOCK, half_units)
    steps = half_units // block
    own = lambda s: jnp.minimum(s, steps - 1)
    other = lambda s: jnp.maximum(s - steps, 0)
    whole = pl.BlockSpec((size, features), lambda s: (0, 0))

    def specs(at):
        return [
            pl.BlockSpec((1, features, block), lambda s: (0, 0, at(s))),
            pl.BlockSpec((1, features, block), lambda s: (0, 0, at(s) + steps)),
            pl.BlockSpec((1, block, features), lambda s: (0, at(s), 0)),
        ]

    count = len(parts)
    return pl.pallas_call(
        functools.partial(expert_body, count, steps),
        grid=(2 * steps,),
        in_specs=[whole] * count + specs(own) + specs(other),
        out_specs=[whole] * count,
        out_shape=[jax.ShapeDtypeStruct((size, features), BF16)] * count,
        scratch_shapes=[pltpu.VMEM((count * size, features), BF16), pltpu.VMEM((count * size, features), F32)],
        cost_estimate=pl.CostEstimate(
            flops=12 * count * size * features * half_units,
            transcendentals=2 * count * size * half_units,
            bytes_accessed=12 * features * half_units + 4 * count * size * features,
        ),
        name="expert",
    )(*parts, w_in, w_in, w_down, other_in, other_in, other_down)


def local(tokens, routes, gates, w_in, w_down):
    plan = Plan(lax.axis_size("expert"), tokens.shape[0])
    routes, gates = routes.T, gates.T
    far_tokens = plan.across(tokens)
    far_routes = plan.across(routes)
    far_gates = plan.across(gates)
    weights = (w_in, w_down, plan.partner(w_in), plan.partner(w_down))
    near_rows = plan.near_exchange(select(plan, routes, tokens))
    far_rows = plan.near_exchange(select(plan, far_routes, far_tokens))
    near_out = expert(near_rows, weights)
    far_out = expert(far_rows, weights)
    far_back = plan.near_exchange(far_out)
    far_sum = plan.across(relay_sum(plan, far_routes, far_gates, far_back))
    near_back = plan.near_exchange(near_out)
    return final_sum(plan, routes, gates, tokens, far_sum, near_back)


def solution(mesh):
    in_specs = (
        P(("groups", "expert"), None),
        P(("groups", "expert"), None),
        P(("groups", "expert"), None),
        P("expert", None, None),
        P("expert", None, None),
    )
    out_specs = P(("groups", "expert"), None)
    return jax.shard_map(local, mesh=mesh, in_specs=in_specs, out_specs=out_specs, check_vma=False)
```

```python
import functools
import jax
import jax.numpy as jnp
from jax import lax
from jax.experimental import pallas as pl
from jax.experimental.pallas import tpu as pltpu
from jax.sharding import PartitionSpec as P


F32 = jnp.float32
BF16 = jnp.bfloat16
GO_WIDTHS = (4, 4)
BACK_WIDTHS = (4, 4)
META_ROWS = 16
HBM = pl.BlockSpec(memory_space=pl.ANY)
VMEM = pl.BlockSpec(memory_space=pltpu.VMEM)
PARAMS = pltpu.CompilerParams(vmem_limit_bytes=16 << 20)


def on_chip(x):
    return pltpu.with_memory_space_constraint(x, pltpu.VMEM)


def spans(widths, features):
    unit = features // sum(widths)
    edges = [unit * sum(widths[:i]) for i in range(len(widths) + 1)]
    return list(zip(edges[:-1], edges[1:]))


def cost(flops, moved):
    return pl.CostEstimate(flops=flops, transcendentals=0, bytes_accessed=moved)


def iota(shape, dim):
    return lax.broadcasted_iota(jnp.int32, shape, dim)


def slot_rows(routes, experts, cap):
    count = routes.shape[1]
    first, second = routes[0:1, :], routes[1:2, :]
    ids = iota((experts, count), 0)
    is_first, is_second = ids == first, ids == second
    named = jnp.where(is_first | is_second, 1.0, 0.0).astype(BF16)
    before = jnp.where(iota((count, count), 0) < iota((count, count), 1), 1.0, 0.0).astype(BF16)
    ranks = jnp.dot(named, before, preferred_element_type=F32)
    rank_first = jnp.sum(jnp.where(is_first, ranks, 0.0), axis=0, keepdims=True)
    rank_second = jnp.sum(jnp.where(is_second, ranks, 0.0), axis=0, keepdims=True)
    return first * cap + rank_first.astype(jnp.int32), second * cap + rank_second.astype(jnp.int32)


class Plan:
    def __init__(self, devices, tok_rows):
        self.devices = devices
        self.experts = devices // 2
        self.cap = min(tok_rows, 4 * tok_rows // self.experts)
        self.near = self.experts // 2
        self.direct = self.near <= 8
        self.pieces = self.near if self.direct else 1
        self.slots = self.near * self.cap
        self.piece_rows = self.slots // self.pieces

    def bases(self):
        me = lax.axis_index("expert")
        chip = me // 2
        half_first = chip // self.near * self.near
        if not self.direct:
            return [half_first * self.cap]
        return [(half_first + ((chip % self.near) ^ j)) * self.cap for j in range(self.pieces)]

    def across(self, x):
        return lax.ppermute(x, "expert", [(i, i ^ self.devices // 2) for i in range(self.devices)])

    def partner(self, x):
        return lax.ppermute(x, "expert", [(i, i ^ 1) for i in range(self.devices)])

    def near_exchange(self, parts):
        if self.direct:
            return [parts[0]] + [
                lax.ppermute(parts[j], "expert", [(i, i ^ 2 * j) for i in range(self.devices)])
                for j in range(1, self.pieces)
            ]
        groups = [
            [2 * (half * self.near + chip) + core for chip in range(self.near)]
            for half in range(2)
            for core in range(2)
        ]
        return [lax.all_to_all(parts[0], "expert", split_axis=0, concat_axis=0, tiled=True, axis_index_groups=groups)]


def picks(plan, first, second):
    slots = iota((plan.piece_rows, first.shape[1]), 0)
    return [
        jnp.where((slots == first - base) | (slots == second - base), 1.0, 0.0).astype(BF16)
        for base in plan.bases()
    ]


def gate_pair(plan, first, second, gates):
    count = first.shape[1]
    rows = jnp.concatenate([first.astype(F32), second.astype(F32), gates, jnp.zeros((124, count), F32)], axis=0)
    columns = rows.T
    first_col = columns[:, 0:1].astype(jnp.int32)
    second_col = columns[:, 1:2].astype(jnp.int32)
    slots = iota((count, plan.piece_rows), 1)
    spread = jnp.concatenate(
        [
            jnp.where(slots == first_col - base, columns[:, 2:3], 0.0)
            + jnp.where(slots == second_col - base, columns[:, 3:4], 0.0)
            for base in plan.bases()
        ],
        axis=1,
    )
    high = spread.astype(BF16)
    return high, (spread - high.astype(F32)).astype(BF16)


def pack_body(routes_ref, gates_ref, tokens_ref, *out_refs):
    count = tokens_ref.shape[0]
    at = 0
    for out_ref in out_refs:
        width = out_ref.shape[1]
        out_ref[0:count, :] = tokens_ref[:, at : at + width]
        at += width
    gates = gates_ref[...]
    high = gates.astype(BF16).astype(F32)
    meta = jnp.concatenate(
        [routes_ref[...].astype(F32), high, gates - high, jnp.zeros((META_ROWS - 6, count), F32)], axis=0
    ).astype(BF16)
    out_refs[0][count : count + META_ROWS, 0:count] = meta
    rest = out_refs[0].shape[1] - count
    if rest:
        out_refs[0][count : count + META_ROWS, count:] = jnp.zeros((META_ROWS, rest), BF16)


def pack(routes, gates, tokens):
    count, features = tokens.shape
    at = spans(GO_WIDTHS, features)
    return pl.pallas_call(
        pack_body,
        in_specs=[VMEM] * 3,
        out_specs=[VMEM] * len(at),
        out_shape=[pltpu.VMEM((count + (META_ROWS if i == 0 else 0), b - a), BF16) for i, (a, b) in enumerate(at)],
        cost_estimate=cost(0, 4 * tokens.size),
        compiler_params=PARAMS,
        name="pack",
    )(routes, gates, tokens)


def select_body(plan, routes_ref, *refs):
    first, second = slot_rows(routes_ref[...], plan.experts, plan.cap)
    chunks, out_refs = refs[: len(GO_WIDTHS)], refs[len(GO_WIDTHS) :]
    count = routes_ref.shape[1]
    for pick, out_ref in zip(picks(plan, first, second), out_refs):
        at = 0
        for chunk in chunks:
            width = chunk.shape[1]
            out_ref[:, at : at + width] = jnp.dot(pick, chunk[0:count, :], preferred_element_type=F32).astype(BF16)
            at += width


def select(plan, routes, chunks):
    features = sum(chunk.shape[1] for chunk in chunks)
    count = routes.shape[1]
    return pl.pallas_call(
        functools.partial(select_body, plan),
        in_specs=[VMEM] * (1 + len(chunks)),
        out_specs=[VMEM] * plan.pieces,
        out_shape=[pltpu.VMEM((plan.piece_rows, features), BF16)] * plan.pieces,
        cost_estimate=cost(2 * plan.slots * count * features, 2 * plan.slots * features),
        compiler_params=PARAMS,
        name="select",
    )(routes, *[on_chip(chunk) for chunk in chunks])


def prepare_body(plan, chunk_ref, pick_ref, high_ref, low_ref):
    count = pick_ref.shape[1]
    meta = chunk_ref[count : count + META_ROWS, 0:count].astype(F32)
    first, second = slot_rows(meta[0:2, :].astype(jnp.int32), plan.experts, plan.cap)
    pick_ref[...] = jnp.concatenate(picks(plan, first, second), axis=0)
    high_ref[...], low_ref[...] = gate_pair(plan, first, second, meta[2:4, :] + meta[4:6, :])


def prepare(plan, count, chunk):
    return pl.pallas_call(
        functools.partial(prepare_body, plan),
        in_specs=[VMEM],
        out_specs=[VMEM] * 3,
        out_shape=[pltpu.VMEM((plan.slots, count), BF16)] + [pltpu.VMEM((count, plan.slots), BF16)] * 2,
        cost_estimate=cost(0, 6 * count * plan.slots),
        compiler_params=PARAMS,
        name="prepare",
    )(on_chip(chunk))


def pick_body(plan, pick_ref, tokens_ref, *out_refs):
    tokens = tokens_ref[0 : pick_ref.shape[1], :]
    for j, out_ref in enumerate(out_refs):
        pick = pick_ref[j * plan.piece_rows : (j + 1) * plan.piece_rows, :]
        out_ref[...] = jnp.dot(pick, tokens, preferred_element_type=F32).astype(BF16)


def pick_rows(plan, pick, chunk):
    width = chunk.shape[1]
    return pl.pallas_call(
        functools.partial(pick_body, plan),
        in_specs=[VMEM] * 2,
        out_specs=[VMEM] * plan.pieces,
        out_shape=[pltpu.VMEM((plan.piece_rows, width), BF16)] * plan.pieces,
        cost_estimate=cost(2 * pick.size * width, 2 * plan.slots * width),
        compiler_params=PARAMS,
        name="pick_rows",
    )(on_chip(pick), on_chip(chunk))


def weigh(high, low, parts):
    return jnp.dot(high, parts, preferred_element_type=F32) + jnp.dot(low, parts, preferred_element_type=F32)


def relay_body(high_ref, low_ref, *refs):
    parts = jnp.concatenate([ref[...] for ref in refs[:-1]], axis=0)
    refs[-1][...] = weigh(high_ref[...], low_ref[...], parts).astype(BF16)


def relay_sum(high, low, parts):
    count, slots = high.shape
    width = parts[0].shape[1]
    return pl.pallas_call(
        relay_body,
        in_specs=[VMEM] * (2 + len(parts)),
        out_specs=VMEM,
        out_shape=pltpu.VMEM((count, width), BF16),
        cost_estimate=cost(4 * count * slots * width, 2 * (slots + count) * width),
        compiler_params=PARAMS,
        name="relay_sum",
    )(on_chip(high), on_chip(low), *[on_chip(part) for part in parts])


def near_sum_body(plan, routes_ref, gates_ref, tokens_ref, after_ref, *refs):
    first, second = slot_rows(routes_ref[...], plan.experts, plan.cap)
    high, low = gate_pair(plan, first, second, gates_ref[...])
    parts = jnp.concatenate([ref[...] for ref in refs[:-1]], axis=0)
    refs[-1][...] = tokens_ref[...].astype(F32) + weigh(high, low, parts)


def near_sum(plan, routes, gates, tokens, parts, after):
    return pl.pallas_call(
        functools.partial(near_sum_body, plan),
        in_specs=[VMEM] * 3 + [HBM] + [VMEM] * len(parts),
        out_specs=VMEM,
        out_shape=pltpu.VMEM(tokens.shape, F32),
        cost_estimate=cost(4 * plan.slots * tokens.size, 10 * tokens.size),
        compiler_params=PARAMS,
        name="near_sum",
    )(routes, gates, tokens, after, *[on_chip(part) for part in parts])


def final_body(base_ref, *refs):
    at = 0
    for ref in refs[:-1]:
        span = slice(at, at + ref.shape[1])
        refs[-1][:, span] = (base_ref[:, span] + ref[...].astype(F32)).astype(BF16)
        at += ref.shape[1]


def final_sum(base, far):
    return pl.pallas_call(
        final_body,
        in_specs=[VMEM] * (1 + len(far)),
        out_specs=VMEM,
        out_shape=jax.ShapeDtypeStruct(base.shape, BF16),
        cost_estimate=cost(2 * base.size, 8 * base.size),
        compiler_params=PARAMS,
        name="final_sum",
    )(on_chip(base), *[on_chip(chunk) for chunk in far])


def expert_body(pieces, chunks_in, chunks_out, *refs):
    parts, refs = refs[: pieces * chunks_in], refs[pieces * chunks_in :]
    weights, refs = refs[:4], refs[5:]
    outs, (rows_ref, acc_ref) = refs[: pieces * chunks_out], refs[pieces * chunks_out :]
    size = parts[0].shape[0]
    half_units = weights[1].shape[1]
    for i in range(pieces):
        at = 0
        for part in parts[i * chunks_in : (i + 1) * chunks_in]:
            rows_ref[i * size : (i + 1) * size, at : at + part.shape[1]] = part[...]
            at += part.shape[1]
    rows = rows_ref[...]
    for w_in, w_down in (weights[:2], weights[2:]):
        gate = jnp.dot(rows, w_in[0, :, 0:half_units], preferred_element_type=F32)
        up = jnp.dot(rows, w_in[0, :, half_units:], preferred_element_type=F32)
        hidden = (jax.nn.silu(gate) * up).astype(BF16)
        partial_value = jnp.dot(hidden, w_down[0], preferred_element_type=F32)
        if w_in is weights[0]:
            acc_ref[...] = partial_value
        else:
            acc_ref[...] += partial_value
    for i in range(pieces):
        at = 0
        for out in outs[i * chunks_out : (i + 1) * chunks_out]:
            out[...] = acc_ref[i * size : (i + 1) * size, at : at + out.shape[1]].astype(BF16)
            at += out.shape[1]


def expert(parts, weights, after, widths):
    pieces, chunks_in, chunks_out = len(parts), len(parts[0]), len(widths)
    size = parts[0][0].shape[0]
    features, half_units = weights[0].shape[1], weights[1].shape[1]
    slots = pieces * size
    outs = pl.pallas_call(
        functools.partial(expert_body, pieces, chunks_in, chunks_out),
        in_specs=[VMEM] * (pieces * chunks_in + 4) + [HBM],
        out_specs=[VMEM] * (pieces * chunks_out),
        out_shape=[pltpu.VMEM((size, b - a), BF16) for a, b in spans(widths, features)] * pieces,
        scratch_shapes=[pltpu.VMEM((slots, features), BF16), pltpu.VMEM((slots, features), F32)],
        cost_estimate=pl.CostEstimate(
            flops=12 * slots * features * half_units,
            transcendentals=2 * slots * half_units,
            bytes_accessed=4 * slots * features,
        ),
        compiler_params=PARAMS,
        name="expert",
    )(*[on_chip(chunk) for piece in parts for chunk in piece], *weights, after)
    return [outs[i * chunks_out : (i + 1) * chunks_out] for i in range(pieces)]


def local(tokens, routes, gates, w_in, w_down):
    plan = Plan(lax.axis_size("expert"), tokens.shape[0])
    routes, gates = routes.T, gates.T
    chunks = pack(routes, gates, tokens)
    far_tokens = [plan.across(chunk) for chunk in chunks]
    weights = [on_chip(w) for w in (w_in, w_down, plan.partner(w_in), plan.partner(w_down))]
    near_rows = plan.near_exchange(select(plan, routes, chunks))
    pick, high, low = prepare(plan, tokens.shape[0], far_tokens[0])
    far_picked = [pick_rows(plan, pick, chunk) for chunk in far_tokens]
    far_rows = [plan.near_exchange(chunk) for chunk in far_picked]
    near_out = expert([[row] for row in near_rows], weights, far_picked[-1][0], (1,))
    far_out = expert([list(row) for row in zip(*far_rows)], weights, near_out[0][0], BACK_WIDTHS)
    near_back = plan.near_exchange([row[0] for row in near_out])
    far_sum = []
    for c in range(len(BACK_WIDTHS)):
        far_back = plan.near_exchange([row[c] for row in far_out])
        far_sum.append(relay_sum(high, low, far_back))
    base = near_sum(plan, routes, gates, tokens, near_back, far_sum[-1])
    return final_sum(base, [plan.across(chunk) for chunk in far_sum])


def solution(mesh):
    in_specs = (
        P(("groups", "expert"), None),
        P(("groups", "expert"), None),
        P(("groups", "expert"), None),
        P("expert", None, None),
        P("expert", None, None),
    )
    out_specs = P(("groups", "expert"), None)
    return jax.shard_map(local, mesh=mesh, in_specs=in_specs, out_specs=out_specs, check_vma=False)
```

```python
import functools
import jax
import jax.numpy as jnp
from jax import lax
from jax.experimental import pallas as pl
from jax.experimental.pallas import tpu as pltpu
from jax.sharding import PartitionSpec as P


F32 = jnp.float32
BF16 = jnp.bfloat16
BACK_WIDTHS = (4, 4)
ANY = pl.BlockSpec(memory_space=pl.ANY)
HBM = pl.BlockSpec(memory_space=pltpu.HBM)
VMEM = pl.BlockSpec(memory_space=pltpu.VMEM)
PARAMS = pltpu.CompilerParams(vmem_limit_bytes=16 << 20)


def on_chip(x):
    return pltpu.with_memory_space_constraint(x, pltpu.VMEM)


def off_chip(x):
    return pltpu.with_memory_space_constraint(x, pltpu.HBM)


def spans(widths, features):
    unit = features // sum(widths)
    edges = [unit * sum(widths[:i]) for i in range(len(widths) + 1)]
    return list(zip(edges[:-1], edges[1:]))


def cost(flops, moved):
    return pl.CostEstimate(flops=flops, transcendentals=0, bytes_accessed=moved)


def iota(shape, dim):
    return lax.broadcasted_iota(jnp.int32, shape, dim)


def slot_rows(routes, experts, cap):
    count = routes.shape[1]
    first, second = routes[0:1, :], routes[1:2, :]
    ids = iota((experts, count), 0)
    is_first, is_second = ids == first, ids == second
    named = jnp.where(is_first | is_second, 1.0, 0.0).astype(BF16)
    before = jnp.where(iota((count, count), 0) < iota((count, count), 1), 1.0, 0.0).astype(BF16)
    ranks = jnp.dot(named, before, preferred_element_type=F32)
    rank_first = jnp.sum(jnp.where(is_first, ranks, 0.0), axis=0, keepdims=True)
    rank_second = jnp.sum(jnp.where(is_second, ranks, 0.0), axis=0, keepdims=True)
    return first * cap + rank_first.astype(jnp.int32), second * cap + rank_second.astype(jnp.int32)


class Plan:
    def __init__(self, devices, tok_rows):
        self.devices = devices
        self.experts = devices // 2
        self.cap = min(tok_rows, 4 * tok_rows // self.experts)
        self.near = self.experts // 2
        self.direct = self.near <= 8
        self.pieces = self.near if self.direct else 1
        self.slots = self.near * self.cap
        self.piece_rows = self.slots // self.pieces

    def bases(self):
        me = lax.axis_index("expert")
        chip = me // 2
        half_first = chip // self.near * self.near
        if not self.direct:
            return [half_first * self.cap]
        return [(half_first + ((chip % self.near) ^ j)) * self.cap for j in range(self.pieces)]

    def across(self, x):
        return lax.ppermute(x, "expert", [(i, i ^ self.devices // 2) for i in range(self.devices)])

    def partner(self, x):
        return lax.ppermute(x, "expert", [(i, i ^ 1) for i in range(self.devices)])

    def near_exchange(self, parts):
        if self.direct:
            return [parts[0]] + [
                lax.ppermute(parts[j], "expert", [(i, i ^ 2 * j) for i in range(self.devices)])
                for j in range(1, self.pieces)
            ]
        groups = [
            [2 * (half * self.near + chip) + core for chip in range(self.near)]
            for half in range(2)
            for core in range(2)
        ]
        return [lax.all_to_all(parts[0], "expert", split_axis=0, concat_axis=0, tiled=True, axis_index_groups=groups)]


def picks(plan, first, second):
    slots = iota((plan.piece_rows, first.shape[1]), 0)
    return [
        jnp.where((slots == first - base) | (slots == second - base), 1.0, 0.0).astype(BF16)
        for base in plan.bases()
    ]


def gate_pair(plan, first, second, gates):
    count = first.shape[1]
    rows = jnp.concatenate([first.astype(F32), second.astype(F32), gates, jnp.zeros((124, count), F32)], axis=0)
    columns = rows.T
    first_col = columns[:, 0:1].astype(jnp.int32)
    second_col = columns[:, 1:2].astype(jnp.int32)
    slots = iota((count, plan.piece_rows), 1)
    spread = jnp.concatenate(
        [
            jnp.where(slots == first_col - base, columns[:, 2:3], 0.0)
            + jnp.where(slots == second_col - base, columns[:, 3:4], 0.0)
            for base in plan.bases()
        ],
        axis=1,
    )
    high = spread.astype(BF16)
    return high, (spread - high.astype(F32)).astype(BF16)


def stage_body(count, *refs):
    sources, outs, sem = refs[:count], refs[count + 1 : 2 * count + 1], refs[-1]
    copies = [pltpu.make_async_copy(sources[i], outs[i], sem.at[i]) for i in range(count)]
    for copy in copies:
        copy.start()
    for copy in copies:
        copy.wait()


def stage(arrays, after):
    return pl.pallas_call(
        functools.partial(stage_body, len(arrays)),
        in_specs=[HBM] * len(arrays) + [ANY],
        out_specs=[VMEM] * len(arrays),
        out_shape=[pltpu.VMEM(x.shape, x.dtype) for x in arrays],
        scratch_shapes=[pltpu.SemaphoreType.DMA((len(arrays),))],
        cost_estimate=cost(0, sum(2 * x.size * x.dtype.itemsize for x in arrays)),
        compiler_params=PARAMS,
        name="stage",
    )(*[off_chip(x) for x in arrays], after)


def select_body(plan, routes_ref, tokens_ref, *refs):
    out_refs, (routes_vmem, tokens_vmem, sem) = refs[:-3], refs[-3:]
    copies = [
        pltpu.make_async_copy(routes_ref, routes_vmem, sem.at[0]),
        pltpu.make_async_copy(tokens_ref, tokens_vmem, sem.at[1]),
    ]
    for copy in copies:
        copy.start()
    copies[0].wait()
    first, second = slot_rows(routes_vmem[...], plan.experts, plan.cap)
    copies[1].wait()
    tokens = tokens_vmem[...]
    for pick, out_ref in zip(picks(plan, first, second), out_refs):
        out_ref[...] = jnp.dot(pick, tokens, preferred_element_type=F32).astype(BF16)


def select(plan, routes, tokens):
    count, features = tokens.shape
    return pl.pallas_call(
        functools.partial(select_body, plan),
        in_specs=[HBM] * 2,
        out_specs=[VMEM] * plan.pieces,
        out_shape=[pltpu.VMEM((plan.piece_rows, features), BF16)] * plan.pieces,
        scratch_shapes=[
            pltpu.VMEM(routes.shape, routes.dtype),
            pltpu.VMEM(tokens.shape, tokens.dtype),
            pltpu.SemaphoreType.DMA((2,)),
        ],
        cost_estimate=cost(2 * plan.slots * count * features, 2 * plan.slots * features),
        compiler_params=PARAMS,
        name="select",
    )(off_chip(routes), off_chip(tokens))


def far_picks_body(plan, routes_ref, after_ref, pick_ref):
    first, second = slot_rows(routes_ref[...], plan.experts, plan.cap)
    pick_ref[...] = jnp.concatenate(picks(plan, first, second), axis=0)


def far_picks(plan, routes, after):
    count = routes.shape[1]
    return pl.pallas_call(
        functools.partial(far_picks_body, plan),
        in_specs=[VMEM, ANY],
        out_specs=VMEM,
        out_shape=pltpu.VMEM((plan.slots, count), BF16),
        cost_estimate=cost(0, 2 * count * plan.slots),
        compiler_params=PARAMS,
        name="far_picks",
    )(on_chip(routes), after)


def far_gates_body(plan, routes_ref, gates_ref, after_ref, high_ref, low_ref):
    first, second = slot_rows(routes_ref[...], plan.experts, plan.cap)
    high_ref[...], low_ref[...] = gate_pair(plan, first, second, gates_ref[...])


def spread_gates(plan, routes, gates, after):
    count = routes.shape[1]
    return pl.pallas_call(
        functools.partial(far_gates_body, plan),
        in_specs=[VMEM] * 2 + [ANY],
        out_specs=[VMEM] * 2,
        out_shape=[pltpu.VMEM((count, plan.slots), BF16)] * 2,
        cost_estimate=cost(0, 4 * count * plan.slots),
        compiler_params=PARAMS,
        name="spread_gates",
    )(on_chip(routes), on_chip(gates), after)


def pick_body(plan, pick_ref, tokens_ref, *out_refs):
    tokens = tokens_ref[...]
    for j, out_ref in enumerate(out_refs):
        pick = pick_ref[j * plan.piece_rows : (j + 1) * plan.piece_rows, :]
        out_ref[...] = jnp.dot(pick, tokens, preferred_element_type=F32).astype(BF16)


def pick_rows(plan, pick, chunk):
    width = chunk.shape[1]
    return pl.pallas_call(
        functools.partial(pick_body, plan),
        in_specs=[VMEM] * 2,
        out_specs=[VMEM] * plan.pieces,
        out_shape=[pltpu.VMEM((plan.piece_rows, width), BF16)] * plan.pieces,
        cost_estimate=cost(2 * pick.size * width, 2 * plan.slots * width),
        compiler_params=PARAMS,
        name="pick_rows",
    )(on_chip(pick), on_chip(chunk))


def weigh(high, low, parts):
    return jnp.dot(high, parts, preferred_element_type=F32) + jnp.dot(low, parts, preferred_element_type=F32)


def relay_body(high_ref, low_ref, *refs):
    parts = jnp.concatenate([ref[...] for ref in refs[:-1]], axis=0)
    refs[-1][...] = weigh(high_ref[...], low_ref[...], parts).astype(BF16)


def relay_sum(high, low, parts):
    count, slots = high.shape
    width = parts[0].shape[1]
    return pl.pallas_call(
        relay_body,
        in_specs=[VMEM] * (2 + len(parts)),
        out_specs=VMEM,
        out_shape=pltpu.VMEM((count, width), BF16),
        cost_estimate=cost(4 * count * slots * width, 2 * (slots + count) * width),
        compiler_params=PARAMS,
        name="relay_sum",
    )(on_chip(high), on_chip(low), *[on_chip(part) for part in parts])


def near_sum_body(plan, routes_ref, gates_ref, tokens_ref, after_ref, *refs):
    first, second = slot_rows(routes_ref[...], plan.experts, plan.cap)
    high, low = gate_pair(plan, first, second, gates_ref[...])
    parts = jnp.concatenate([ref[...] for ref in refs[:-1]], axis=0)
    refs[-1][...] = tokens_ref[...].astype(F32) + weigh(high, low, parts)


def near_sum(plan, routes, gates, tokens, parts, after):
    return pl.pallas_call(
        functools.partial(near_sum_body, plan),
        in_specs=[VMEM] * 3 + [ANY] + [VMEM] * len(parts),
        out_specs=VMEM,
        out_shape=pltpu.VMEM(tokens.shape, F32),
        cost_estimate=cost(4 * plan.slots * tokens.size, 10 * tokens.size),
        compiler_params=PARAMS,
        name="near_sum",
    )(routes, gates, tokens, after, *[on_chip(part) for part in parts])


def final_body(base_ref, *refs):
    at = 0
    for ref in refs[:-1]:
        span = slice(at, at + ref.shape[1])
        refs[-1][:, span] = (base_ref[:, span] + ref[...].astype(F32)).astype(BF16)
        at += ref.shape[1]


def final_sum(base, far):
    return pl.pallas_call(
        final_body,
        in_specs=[VMEM] * (1 + len(far)),
        out_specs=VMEM,
        out_shape=jax.ShapeDtypeStruct(base.shape, BF16),
        cost_estimate=cost(2 * base.size, 8 * base.size),
        compiler_params=PARAMS,
        name="final_sum",
    )(on_chip(base), *[on_chip(chunk) for chunk in far])


def hidden_units(rows, w_in, half_units):
    gate = jnp.dot(rows, w_in[0, :, 0:half_units], preferred_element_type=F32)
    up = jnp.dot(rows, w_in[0, :, half_units:], preferred_element_type=F32)
    return (jax.nn.silu(gate) * up).astype(BF16)


def down_sum(hidden, downs, at):
    partials = [jnp.dot(h, down[0, :, at], preferred_element_type=F32) for h, down in zip(hidden, downs)]
    return (partials[0] + partials[1]).astype(BF16)


def expert_body(pieces, *refs):
    parts, refs = refs[:pieces], refs[pieces:]
    (in_a, down_a, in_b, down_b, _), refs = refs[:5], refs[5:]
    outs, (hid_a, hid_b) = refs[:pieces], refs[pieces : pieces + 2]
    size, width = outs[0].shape
    half_units = down_a.shape[1]
    rows = jnp.concatenate([part[...] for part in parts], axis=0)
    hid_a[...] = hidden_units(rows, in_a, half_units)
    hid_b[...] = hidden_units(rows, in_b, half_units)
    total = down_sum((hid_a[...], hid_b[...]), (down_a, down_b), slice(0, width))
    for i, out in enumerate(outs):
        out[...] = total[i * size : (i + 1) * size, :]


def expert(parts, weights, after, width):
    pieces = len(parts)
    size = parts[0].shape[0]
    features, half_units = weights[0].shape[1], weights[1].shape[1]
    slots = pieces * size
    outs = pl.pallas_call(
        functools.partial(expert_body, pieces),
        in_specs=[VMEM] * (pieces + 4) + [ANY],
        out_specs=[VMEM] * (pieces + 2),
        out_shape=[pltpu.VMEM((size, width), BF16)] * pieces + [pltpu.VMEM((slots, half_units), BF16)] * 2,
        cost_estimate=pl.CostEstimate(
            flops=4 * slots * half_units * (2 * features + width),
            transcendentals=2 * slots * half_units,
            bytes_accessed=2 * slots * (features + width),
        ),
        compiler_params=PARAMS,
    )(*[on_chip(part) for part in parts], *weights, after)
    return outs[:pieces], outs[pieces:]


def rest_body(pieces, hid_a, hid_b, down_a, down_b, *outs):
    size = outs[0].shape[0]
    at = down_a.shape[2] - sum(out.shape[1] for out in outs[::pieces])
    for c in range(len(outs) // pieces):
        width = outs[c * pieces].shape[1]
        total = down_sum((hid_a[...], hid_b[...]), (down_a, down_b), slice(at, at + width))
        for i in range(pieces):
            outs[c * pieces + i][...] = total[i * size : (i + 1) * size, :]
        at += width


def expert_rest(hidden, weights, pieces, widths):
    slots, half_units = hidden[0].shape
    size = slots // pieces
    outs = pl.pallas_call(
        functools.partial(rest_body, pieces),
        in_specs=[VMEM] * 4,
        out_specs=[VMEM] * (pieces * len(widths)),
        out_shape=[pltpu.VMEM((size, width), BF16) for width in widths for _ in range(pieces)],
        cost_estimate=cost(4 * slots * half_units * sum(widths), 2 * slots * sum(widths)),
        compiler_params=PARAMS,
        name="far_rest",
    )(*[on_chip(x) for x in hidden], weights[1], weights[3])
    return [outs[c * pieces : (c + 1) * pieces] for c in range(len(widths))]


def local(tokens, routes, gates, w_in, w_down):
    plan = Plan(lax.axis_size("expert"), tokens.shape[0])
    features = tokens.shape[1]
    routes, gates = routes.T, gates.T
    far_routes = plan.across(routes)
    far_tokens = plan.across(tokens)
    far_gates = plan.across(gates)
    partner = [on_chip(plan.partner(w)) for w in (w_in, w_down)]
    near_picked = select(plan, routes, tokens)
    near_rows = plan.near_exchange(near_picked)
    weights = list(stage((w_in, w_down), near_picked[0])) + partner
    pick = far_picks(plan, far_routes, weights[1])
    far_picked = pick_rows(plan, pick, far_tokens)
    far_rows = plan.near_exchange(far_picked)
    near_out, _ = expert(near_rows, weights, far_picked[0], features)
    near_back = plan.near_exchange(near_out)
    high, low = spread_gates(plan, far_routes, far_gates, near_out[0])
    widths = [b - a for a, b in spans(BACK_WIDTHS, features)]
    first_out, hidden = expert(far_rows, weights, high, widths[0])
    far_out = [first_out] + expert_rest(hidden, weights, plan.pieces, widths[1:])
    far_total = []
    for c in range(len(widths)):
        far_back = plan.near_exchange(far_out[c])
        far_sum = relay_sum(high, low, far_back)
        far_total.append(plan.across(far_sum))
    base = near_sum(plan, routes, gates, tokens, near_back, far_sum)
    return final_sum(base, far_total)


def solution(mesh):
    in_specs = (
        P(("groups", "expert"), None),
        P(("groups", "expert"), None),
        P(("groups", "expert"), None),
        P("expert", None, None),
        P("expert", None, None),
    )
    out_specs = P(("groups", "expert"), None)

    return jax.shard_map(local, mesh=mesh, in_specs=in_specs, out_specs=out_specs, check_vma=False)
```

```python
import functools
import jax
import jax.numpy as jnp
from jax import lax
from jax.experimental import pallas as pl
from jax.experimental.pallas import tpu as pltpu
from jax.sharding import PartitionSpec as P


F32 = jnp.float32
BF16 = jnp.bfloat16
BACK_WIDTHS = (4, 4)
DOWN_BLOCK = 512
ANY = pl.BlockSpec(memory_space=pl.ANY)
HBM = pl.BlockSpec(memory_space=pltpu.HBM)
VMEM = pl.BlockSpec(memory_space=pltpu.VMEM)
PARAMS = pltpu.CompilerParams(vmem_limit_bytes=16 << 20)


def on_chip(x):
    return pltpu.with_memory_space_constraint(x, pltpu.VMEM)


def off_chip(x):
    return pltpu.with_memory_space_constraint(x, pltpu.HBM)


def spans(widths, features):
    unit = features // sum(widths)
    edges = [unit * sum(widths[:i]) for i in range(len(widths) + 1)]
    return list(zip(edges[:-1], edges[1:]))


def cost(flops, moved):
    return pl.CostEstimate(flops=flops, transcendentals=0, bytes_accessed=moved)


def iota(shape, dim):
    return lax.broadcasted_iota(jnp.int32, shape, dim)


def slot_rows(routes, experts, cap):
    count = routes.shape[1]
    first, second = routes[0:1, :], routes[1:2, :]
    ids = iota((experts, count), 0)
    is_first, is_second = ids == first, ids == second
    named = jnp.where(is_first | is_second, 1.0, 0.0).astype(BF16)
    before = jnp.where(iota((count, count), 0) < iota((count, count), 1), 1.0, 0.0).astype(BF16)
    ranks = jnp.dot(named, before, preferred_element_type=F32)
    rank_first = jnp.sum(jnp.where(is_first, ranks, 0.0), axis=0, keepdims=True)
    rank_second = jnp.sum(jnp.where(is_second, ranks, 0.0), axis=0, keepdims=True)
    return first * cap + rank_first.astype(jnp.int32), second * cap + rank_second.astype(jnp.int32)


class Plan:
    def __init__(self, devices, tok_rows):
        self.devices = devices
        self.experts = devices // 2
        self.cap = min(tok_rows, 4 * tok_rows // self.experts)
        self.near = self.experts // 2
        self.direct = self.near <= 8
        self.pieces = self.near if self.direct else 1
        self.slots = self.near * self.cap
        self.piece_rows = self.slots // self.pieces

    def bases(self):
        me = lax.axis_index("expert")
        chip = me // 2
        half_first = chip // self.near * self.near
        if not self.direct:
            return [half_first * self.cap]
        return [(half_first + ((chip % self.near) ^ j)) * self.cap for j in range(self.pieces)]

    def across(self, x):
        return lax.ppermute(x, "expert", [(i, i ^ self.devices // 2) for i in range(self.devices)])

    def partner(self, x):
        return lax.ppermute(x, "expert", [(i, i ^ 1) for i in range(self.devices)])

    def near_exchange(self, parts):
        if self.direct:
            got = [parts[0]]
            for j in range(1, self.pieces):
                got.append(lax.ppermute(parts[j], "expert", [(i, i ^ 2 * j) for i in range(self.devices)]))
            return got
        groups = [
            [2 * (half * self.near + chip) + core for chip in range(self.near)]
            for half in range(2)
            for core in range(2)
        ]
        return [lax.all_to_all(parts[0], "expert", split_axis=0, concat_axis=0, tiled=True, axis_index_groups=groups)]


def picks(plan, first, second):
    slots = iota((plan.piece_rows, first.shape[1]), 0)
    return [
        jnp.where((slots == first - base) | (slots == second - base), 1.0, 0.0).astype(BF16)
        for base in plan.bases()
    ]


def gate_pair(plan, first, second, gates):
    count = first.shape[1]
    rows = jnp.concatenate([first.astype(F32), second.astype(F32), gates, jnp.zeros((124, count), F32)], axis=0)
    columns = rows.T
    first_col = columns[:, 0:1].astype(jnp.int32)
    second_col = columns[:, 1:2].astype(jnp.int32)
    slots = iota((count, plan.piece_rows), 1)
    spread = jnp.concatenate(
        [
            jnp.where(slots == first_col - base, columns[:, 2:3], 0.0)
            + jnp.where(slots == second_col - base, columns[:, 3:4], 0.0)
            for base in plan.bases()
        ],
        axis=1,
    )
    high = spread.astype(BF16)
    return high, (spread - high.astype(F32)).astype(BF16)


def stage_body(count, *refs):
    sources, outs, sem = refs[:count], refs[count + 1 : 2 * count + 1], refs[-1]
    copies = [pltpu.make_async_copy(sources[i], outs[i], sem.at[i]) for i in range(count)]
    for copy in copies:
        copy.start()
    for copy in copies:
        copy.wait()


def stage(arrays, after):
    return pl.pallas_call(
        functools.partial(stage_body, len(arrays)),
        in_specs=[HBM] * len(arrays) + [ANY],
        out_specs=[VMEM] * len(arrays),
        out_shape=[pltpu.VMEM(x.shape, x.dtype) for x in arrays],
        scratch_shapes=[pltpu.SemaphoreType.DMA((len(arrays),))],
        cost_estimate=cost(0, sum(2 * x.size * x.dtype.itemsize for x in arrays)),
        compiler_params=PARAMS,
        name="stage",
    )(*[off_chip(x) for x in arrays], after)


def select_body(plan, routes_ref, tokens_ref, *refs):
    out_refs, (routes_vmem, tokens_vmem, sem) = refs[:-3], refs[-3:]
    copies = [
        pltpu.make_async_copy(routes_ref, routes_vmem, sem.at[0]),
        pltpu.make_async_copy(tokens_ref, tokens_vmem, sem.at[1]),
    ]
    for copy in copies:
        copy.start()
    copies[0].wait()
    first, second = slot_rows(routes_vmem[...], plan.experts, plan.cap)
    copies[1].wait()
    tokens = tokens_vmem[...]
    for pick, out_ref in zip(picks(plan, first, second), out_refs):
        out_ref[...] = jnp.dot(pick, tokens, preferred_element_type=F32).astype(BF16)


def select(plan, routes, tokens):
    count, features = tokens.shape
    return pl.pallas_call(
        functools.partial(select_body, plan),
        in_specs=[HBM] * 2,
        out_specs=[VMEM] * plan.pieces,
        out_shape=[pltpu.VMEM((plan.piece_rows, features), BF16)] * plan.pieces,
        scratch_shapes=[
            pltpu.VMEM(routes.shape, routes.dtype),
            pltpu.VMEM(tokens.shape, tokens.dtype),
            pltpu.SemaphoreType.DMA((2,)),
        ],
        cost_estimate=cost(2 * plan.slots * count * features, 2 * plan.slots * features),
        compiler_params=PARAMS,
        name="select",
    )(off_chip(routes), off_chip(tokens))


def far_picks_body(plan, routes_ref, after_ref, pick_ref):
    first, second = slot_rows(routes_ref[...], plan.experts, plan.cap)
    pick_ref[...] = jnp.concatenate(picks(plan, first, second), axis=0)


def far_picks(plan, routes, after):
    count = routes.shape[1]
    return pl.pallas_call(
        functools.partial(far_picks_body, plan),
        in_specs=[VMEM, ANY],
        out_specs=VMEM,
        out_shape=pltpu.VMEM((plan.slots, count), BF16),
        cost_estimate=cost(0, 2 * count * plan.slots),
        compiler_params=PARAMS,
        name="far_picks",
    )(on_chip(routes), after)


def far_gates_body(plan, routes_ref, gates_ref, after_ref, high_ref, low_ref):
    first, second = slot_rows(routes_ref[...], plan.experts, plan.cap)
    high_ref[...], low_ref[...] = gate_pair(plan, first, second, gates_ref[...])


def spread_gates(plan, routes, gates, after):
    count = routes.shape[1]
    return pl.pallas_call(
        functools.partial(far_gates_body, plan),
        in_specs=[VMEM] * 2 + [ANY],
        out_specs=[VMEM] * 2,
        out_shape=[pltpu.VMEM((count, plan.slots), BF16)] * 2,
        cost_estimate=cost(0, 4 * count * plan.slots),
        compiler_params=PARAMS,
        name="spread_gates",
    )(on_chip(routes), on_chip(gates), after)


def pick_body(plan, pick_ref, tokens_ref, *out_refs):
    tokens = tokens_ref[...]
    for j, out_ref in enumerate(out_refs):
        pick = pick_ref[j * plan.piece_rows : (j + 1) * plan.piece_rows, :]
        out_ref[...] = jnp.dot(pick, tokens, preferred_element_type=F32).astype(BF16)


def pick_rows(plan, pick, chunk):
    width = chunk.shape[1]
    return pl.pallas_call(
        functools.partial(pick_body, plan),
        in_specs=[VMEM] * 2,
        out_specs=[VMEM] * plan.pieces,
        out_shape=[pltpu.VMEM((plan.piece_rows, width), BF16)] * plan.pieces,
        cost_estimate=cost(2 * pick.size * width, 2 * plan.slots * width),
        compiler_params=PARAMS,
        name="pick_rows",
    )(on_chip(pick), on_chip(chunk))


def weigh(high, low, parts):
    return jnp.dot(high, parts, preferred_element_type=F32) + jnp.dot(low, parts, preferred_element_type=F32)


def relay_body(high_ref, low_ref, *refs):
    parts = jnp.concatenate([ref[...] for ref in refs[:-1]], axis=0)
    refs[-1][...] = weigh(high_ref[...], low_ref[...], parts).astype(BF16)


def relay_sum(high, low, parts):
    count, slots = high.shape
    width = parts[0].shape[1]
    return pl.pallas_call(
        relay_body,
        in_specs=[VMEM] * (2 + len(parts)),
        out_specs=VMEM,
        out_shape=pltpu.VMEM((count, width), BF16),
        cost_estimate=cost(4 * count * slots * width, 2 * (slots + count) * width),
        compiler_params=PARAMS,
        name="relay_sum",
    )(on_chip(high), on_chip(low), *[on_chip(part) for part in parts])


def near_sum_body(plan, routes_ref, gates_ref, tokens_ref, after_ref, *refs):
    first, second = slot_rows(routes_ref[...], plan.experts, plan.cap)
    high, low = gate_pair(plan, first, second, gates_ref[...])
    parts = jnp.concatenate([ref[...] for ref in refs[:-1]], axis=0)
    refs[-1][...] = tokens_ref[...].astype(F32) + weigh(high, low, parts)


def near_sum(plan, routes, gates, tokens, parts, after):
    return pl.pallas_call(
        functools.partial(near_sum_body, plan),
        in_specs=[VMEM] * 3 + [ANY] + [VMEM] * len(parts),
        out_specs=VMEM,
        out_shape=pltpu.VMEM(tokens.shape, F32),
        cost_estimate=cost(4 * plan.slots * tokens.size, 10 * tokens.size),
        compiler_params=PARAMS,
        name="near_sum",
    )(routes, gates, tokens, after, *[on_chip(part) for part in parts])


def final_body(base_ref, *refs):
    at = 0
    for ref in refs[:-1]:
        span = slice(at, at + ref.shape[1])
        refs[-1][:, span] = (base_ref[:, span] + ref[...].astype(F32)).astype(BF16)
        at += ref.shape[1]


def final_sum(base, far):
    return pl.pallas_call(
        final_body,
        in_specs=[VMEM] * (1 + len(far)),
        out_specs=VMEM,
        out_shape=jax.ShapeDtypeStruct(base.shape, BF16),
        cost_estimate=cost(2 * base.size, 8 * base.size),
        compiler_params=PARAMS,
        name="final_sum",
    )(on_chip(base), *[on_chip(chunk) for chunk in far])


def hidden_units(rows, w_in, half_units):
    gate = jnp.dot(rows, w_in[0, :, 0:half_units], preferred_element_type=F32)
    up = jnp.dot(rows, w_in[0, :, half_units:], preferred_element_type=F32)
    return (jax.nn.silu(gate) * up).astype(BF16)


def down_sum(hidden, downs, at):
    partials = [jnp.dot(h, down[0, :, at], preferred_element_type=F32) for h, down in zip(hidden, downs)]
    return (partials[0] + partials[1]).astype(BF16)


def expert_body(pieces, chunks, *refs):
    parts, refs = refs[:pieces], refs[pieces:]
    (in_a, down_a, in_b, down_b, _), refs = refs[:5], refs[5:]
    outs, (hid_a, hid_b) = refs[: chunks * pieces], refs[chunks * pieces :]
    size = outs[0].shape[0]
    half_units = down_a.shape[1]
    rows = jnp.concatenate([part[...] for part in parts], axis=0)
    hid_a[...] = hidden_units(rows, in_a, half_units)
    hid_b[...] = hidden_units(rows, in_b, half_units)
    at = 0
    for c in range(chunks):
        width = outs[c * pieces].shape[1]
        step = min(width, DOWN_BLOCK)
        for low in range(0, width, step):
            total = down_sum((hid_a[...], hid_b[...]), (down_a, down_b), slice(at + low, at + low + step))
            for i in range(pieces):
                outs[c * pieces + i][:, low : low + step] = total[i * size : (i + 1) * size, :]
        at += width


def expert(parts, weights, after, widths, keep=False):
    pieces, chunks = len(parts), len(widths)
    size = parts[0].shape[0]
    features, half_units = weights[0].shape[1], weights[1].shape[1]
    slots = pieces * size
    hidden = [pltpu.VMEM((slots, half_units), BF16)] * 2
    outs = pl.pallas_call(
        functools.partial(expert_body, pieces, chunks),
        in_specs=[VMEM] * (pieces + 4) + [ANY],
        out_specs=[VMEM] * (pieces * chunks + (2 if keep else 0)),
        out_shape=[pltpu.VMEM((size, width), BF16) for width in widths for _ in range(pieces)] + (hidden if keep else []),
        scratch_shapes=[] if keep else hidden,
        cost_estimate=pl.CostEstimate(
            flops=4 * slots * half_units * (2 * features + sum(widths)),
            transcendentals=2 * slots * half_units,
            bytes_accessed=2 * slots * (features + sum(widths)),
        ),
        compiler_params=PARAMS,
    )(*[on_chip(part) for part in parts], *weights, after)
    return [outs[c * pieces : (c + 1) * pieces] for c in range(chunks)], outs[chunks * pieces :]


def rest_body(pieces, hid_a, hid_b, down_a, down_b, *outs):
    size = outs[0].shape[0]
    at = down_a.shape[2] - sum(out.shape[1] for out in outs[::pieces])
    for c in range(len(outs) // pieces):
        width = outs[c * pieces].shape[1]
        total = down_sum((hid_a[...], hid_b[...]), (down_a, down_b), slice(at, at + width))
        for i in range(pieces):
            outs[c * pieces + i][...] = total[i * size : (i + 1) * size, :]
        at += width


def expert_rest(hidden, weights, pieces, widths):
    slots, half_units = hidden[0].shape
    size = slots // pieces
    outs = pl.pallas_call(
        functools.partial(rest_body, pieces),
        in_specs=[VMEM] * 4,
        out_specs=[VMEM] * (pieces * len(widths)),
        out_shape=[pltpu.VMEM((size, width), BF16) for width in widths for _ in range(pieces)],
        cost_estimate=cost(4 * slots * half_units * sum(widths), 2 * slots * sum(widths)),
        compiler_params=PARAMS,
        name="far_rest",
    )(*[on_chip(x) for x in hidden], weights[1], weights[3])
    return [outs[c * pieces : (c + 1) * pieces] for c in range(len(widths))]


def local(tokens, routes, gates, w_in, w_down):
    plan = Plan(lax.axis_size("expert"), tokens.shape[0])
    features = tokens.shape[1]
    routes, gates = routes.T, gates.T
    far_routes = plan.across(routes)
    far_tokens = plan.across(tokens)
    far_gates = plan.across(gates)
    partner = [on_chip(plan.partner(w)) for w in (w_in, w_down)]
    near_picked = select(plan, routes, tokens)
    near_rows = plan.near_exchange(near_picked)
    weights = list(stage((w_in, w_down), near_picked[0])) + partner
    widths = [b - a for a, b in spans(BACK_WIDTHS, features)]
    early = plan.pieces // 2
    near_early, after = [], weights[1]
    if early:
        (near_early,), _ = expert(near_rows[:early], weights, after, (features,))
        after = near_early[0]
    pick = far_picks(plan, far_routes, after)
    far_picked = pick_rows(plan, pick, far_tokens)
    far_rows = plan.near_exchange(far_picked)
    (near_late,), _ = expert(near_rows[early:], weights, far_picked[0], (features,))
    near_back = plan.near_exchange(list(near_early) + list(near_late))
    far_early, after = [[] for _ in widths], near_late[0]
    if early:
        far_early, _ = expert(far_rows[:early], weights, after, widths)
        after = far_early[0][0]
    (first_out,), hidden = expert(far_rows[early:], weights, after, widths[:1], keep=True)
    high, low = spread_gates(plan, far_routes, far_gates, first_out[0])
    far_late = [first_out] + expert_rest(hidden, weights, plan.pieces - early, widths[1:])
    far_total = []
    for c in range(len(widths)):
        far_back = plan.near_exchange(list(far_early[c]) + list(far_late[c]))
        far_sum = relay_sum(high, low, far_back)
        far_total.append(plan.across(far_sum))
    base = near_sum(plan, routes, gates, tokens, near_back, far_sum)
    return final_sum(base, far_total)


def solution(mesh):
    in_specs = (
        P(("groups", "expert"), None),
        P(("groups", "expert"), None),
        P(("groups", "expert"), None),
        P("expert", None, None),
        P("expert", None, None),
    )
    out_specs = P(("groups", "expert"), None)

    return jax.shard_map(local, mesh=mesh, in_specs=in_specs, out_specs=out_specs, check_vma=False)
```
